32 devices in a mesh: seq: 8 (over z, x), head: 4 (over y, core).
Axes of the slice: x: 2, y: 2, z: 4, core: 2. Of those that a mesh axis runs over, the one named last changes fastest.
Arguments:
- inputs: bfloat16 [3, 4096, 4096], P(None, 'seq', 'head'), may hold values from -11 to 11
- conv_weight: float32 [3, 3, 4096], P(None, None, 'head'), may hold values from -9 to 9
- gain: float32 [4096], P('head'), may hold values from 0.5 to 1.5
- cotangent: bfloat16 [4096, 4096], P('seq', 'head'), may hold values from -11 to 11
Outputs:
- output: bfloat16 [4096, 4096], P('seq', 'head')
- grad_inputs: bfloat16 [3, 4096, 4096], P(None, 'seq', 'head')
The draws below stay inside these ranges and needn't reach their ends.
All inputs are finite; a program needn't handle non-finite values.
Results may differ from the reference program's by a relative error of at most 0.0078.
Values may be sent and summed in bfloat16 or wider, within the bound.
A program may use at most 128 MiB of HBM per device.

```python
import jax
import jax.numpy as jnp
from jax import lax

WIDTH = 4096
HEADS = 32
HEAD_DIM = 128
CONV = 3
BLOCK = 512
SEQ_LEN = 4096


def drawn_field(key, shape):
    return jnp.clip(jax.random.normal(key, shape, jnp.float32), -4.0, 4.0)


def draw_inputs(key, part):
    shape = (3, SEQ_LEN, WIDTH)
    field = drawn_field(jax.random.fold_in(key, 11), shape)
    return field.astype(jnp.bfloat16)


def draw_cotangent(key, part):
    shape = (SEQ_LEN, WIDTH)
    field = drawn_field(jax.random.fold_in(key, 23), shape)
    return field.astype(jnp.bfloat16)


def draw_conv_weight(key, part):
    shape = (3, CONV, WIDTH)
    head_pos = (jnp.arange(WIDTH) // HEAD_DIM).astype(jnp.float32) / max(HEADS - 1, 1)
    stream_pos = jnp.arange(3)[:, None, None]
    sample_key = jax.random.fold_in(key, 37)
    base = 0.5 * jnp.clip(jax.random.normal(sample_key, shape, jnp.float32), -4.0, 4.0)
    factor = jnp.where(stream_pos == 2, 1.0 + 2.0 * head_pos[None, None, :], 1.0)
    return (base * factor).astype(jnp.float32)


def setup_inputs(seed: int = 0) -> dict:
    key_list = jax.random.split(jax.random.key(seed), 5)
    return {
        "inputs": draw_inputs(jax.random.fold_in(key_list[4], 71), 0),
        "conv_weight": draw_conv_weight(jax.random.fold_in(key_list[4], 71), 0),
        "gain": jnp.clip(1.0 + 0.1 * jax.random.normal(key_list[2], (WIDTH,), jnp.float32), 0.5, 1.5),
        "cotangent": draw_cotangent(jax.random.fold_in(key_list[4], 71), 0),
    }


def convolve_forward(inputs, conv_weight):
    streams = []
    for stream in range(3):
        padded = jnp.pad(inputs[stream].astype(jnp.float32), ((CONV - 1, 0), (0, 0)))
        total = jnp.zeros((SEQ_LEN, WIDTH), jnp.float32)
        for offset in range(CONV):
            total = total + conv_weight[stream, offset][None, :] * padded[CONV - 1 - offset:CONV - 1 - offset + SEQ_LEN]
        streams.append(total.astype(jnp.bfloat16))
    return streams

def convolve_backward(grads, conv_weight):
    streams = []
    for stream in range(3):
        padded = jnp.pad(grads[stream].astype(jnp.float32), ((0, CONV - 1), (0, 0)))
        total = jnp.zeros((SEQ_LEN, WIDTH), jnp.float32)
        for offset in range(CONV):
            total = total + conv_weight[stream, offset][None, :] * padded[offset:offset + SEQ_LEN]
        streams.append(total.astype(jnp.bfloat16))
    return jnp.stack(streams)

def reference(inputs, conv_weight, gain, cotangent):
    count = SEQ_LEN // BLOCK
    queries, key_rows, values = convolve_forward(inputs, conv_weight)

    def by_blocks(array):
        return array.reshape(count, BLOCK, HEADS, HEAD_DIM)
    causal = jnp.tril(jnp.ones((BLOCK, BLOCK), dtype=bool))

    def forward_step(state, pieces):
        q_rows, k_rows, v_rows = pieces
        state_bf = state.astype(jnp.bfloat16)
        scores = jnp.einsum('thd,shd->hts', q_rows.astype(jnp.float32), k_rows.astype(jnp.float32))
        scores = jnp.where(causal[None], scores, 0.0).astype(jnp.bfloat16)
        attended = jnp.einsum('thd,hde->the', q_rows.astype(jnp.float32), state_bf.astype(jnp.float32))
        attended = attended + jnp.einsum('hts,she->the', scores.astype(jnp.float32), v_rows.astype(jnp.float32))
        state_next = state + jnp.einsum('shd,she->hde', k_rows.astype(jnp.float32), v_rows.astype(jnp.float32))
        return (state_next, (attended, state))
    start = jnp.zeros((HEADS, HEAD_DIM, HEAD_DIM), jnp.float32)
    final_state, (attended_blocks, states) = lax.scan(forward_step, start, (by_blocks(queries), by_blocks(key_rows), by_blocks(values)))
    attended = attended_blocks.reshape(SEQ_LEN, WIDTH)
    rms = jnp.sqrt(lax.optimization_barrier(jnp.mean(attended * attended, axis=-1)) + 1e-05)
    output = (gain[None, :] * attended / rms[:, None]).astype(jnp.bfloat16)
    weighted = gain[None, :] * cotangent.astype(jnp.float32)
    inner = lax.optimization_barrier(jnp.sum(weighted * attended, axis=-1))
    grad_attended = (weighted / rms[:, None] - attended * (inner / (WIDTH * rms * rms * rms))[:, None]).astype(jnp.bfloat16)

    def backward_step(after, pieces):
        q_rows, k_rows, v_rows, g_rows, state = pieces
        after_bf = after.astype(jnp.bfloat16)
        state_bf = state.astype(jnp.bfloat16)
        q32 = q_rows.astype(jnp.float32)
        k32 = k_rows.astype(jnp.float32)
        v32 = v_rows.astype(jnp.float32)
        g32 = g_rows.astype(jnp.float32)
        scores = jnp.where(causal[None], jnp.einsum('thd,shd->hts', q32, k32), 0.0).astype(jnp.bfloat16)
        mixed = jnp.where(causal[None], jnp.einsum('the,she->hts', g32, v32), 0.0).astype(jnp.bfloat16)
        mixed32 = mixed.astype(jnp.float32)
        grad_q = jnp.einsum('the,hde->thd', g32, state_bf.astype(jnp.float32)) + jnp.einsum('hts,shd->thd', mixed32, k32)
        grad_k = jnp.einsum('she,hde->shd', v32, after_bf.astype(jnp.float32)) + jnp.einsum('hts,thd->shd', mixed32, q32)
        grad_v = jnp.einsum('shd,hde->she', k32, after_bf.astype(jnp.float32)) + jnp.einsum('hts,the->she', scores.astype(jnp.float32), g32)
        after_next = after + jnp.einsum('thd,the->hde', q32, g32)
        return (after_next, (grad_q, grad_k, grad_v))
    last = jnp.zeros((HEADS, HEAD_DIM, HEAD_DIM), jnp.float32)
    first_after, (grad_q, grad_k, grad_v) = lax.scan(backward_step, last, (by_blocks(queries), by_blocks(key_rows), by_blocks(values), by_blocks(grad_attended), states), reverse=True)
    grads = [piece.reshape(SEQ_LEN, WIDTH).astype(jnp.bfloat16) for piece in (grad_q, grad_k, grad_v)]
    grad_inputs = convolve_backward(grads, conv_weight)
    return (output, grad_inputs)
```

```python
import jax
import jax.numpy as jnp
from jax import lax
from jax.experimental import pallas as pl
from jax.experimental.pallas import tpu as pltpu
from jax.sharding import PartitionSpec as P

HEAD_DIM = 128
BLOCK = 512
RIM = 8
TAIL = 16
F32 = jnp.float32
BF16 = jnp.bfloat16
MESH = pl.DeviceIdType.MESH


def dot(a, b, ca, cb):
    return lax.dot_general(a, b, (((ca,), (cb,)), ((), ())), preferred_element_type=F32)


def split_of(count):
    inner = 1
    while inner * inner * 4 <= count and count % (inner * 2) == 0:
        inner *= 2
    return count // inner, inner


def lower_mask(rows, cols, shift):
    return lax.broadcasted_iota(jnp.int32, (rows, cols), 0) + shift >= lax.broadcasted_iota(
        jnp.int32, (rows, cols), 1
    )


def upper_mask(rows, cols):
    return lax.broadcasted_iota(jnp.int32, (rows, cols), 0) <= lax.broadcasted_iota(
        jnp.int32, (rows, cols), 1
    )


def make_kernel(n_seq, n_head, rows, cols, taps):
    outer, inner = split_of(n_seq)
    heads = cols // HEAD_DIM
    width = cols * n_head
    half = rows // 2
    groups = rows // HEAD_DIM

    def kernel(
        x_hbm, w_ref, gain_ref, c_hbm, out_hbm, gi_hbm,
        xin, cin, qkv, xs, left, scT, att, stb, s_acc, i_acc,
        stat_s, stat_r, rb, cb, gb, outb, gq, gkv, tail, gib,
        own, xsend, xrecv, zsend, zrecv, hsend, hrecv,
        in_sem, c_sem, out_sem, gi_sem, tail_sem, lsem, xsem_s, xsem_r, zsem_s, zsem_r,
        ssem_s, ssem_r, hsem_s, hsem_r,
    ):
        me = lax.axis_index("seq")
        hd = lax.axis_index("head")
        z = me // inner
        x = lax.rem(me, inner)

        def col(h):
            return pl.ds(pl.multiple_of(h * HEAD_DIM, HEAD_DIM), HEAD_DIM)

        def in_copy(h):
            return pltpu.make_async_copy(
                x_hbm.at[:, :, col(h)], xin.at[:, :, col(h)], in_sem.at[h]
            )

        c_copy = pltpu.make_async_copy(c_hbm, cin, c_sem)

        @pl.loop(0, heads)
        def _(h):
            in_copy(h).start()

        c_copy.start()

        bar = pltpu.get_barrier_semaphore()

        def greet(seq, head):
            pl.semaphore_signal(bar, inc=1, device_id=(seq, head), device_id_type=MESH)

        def peer_x(d):
            return z * inner + lax.rem(x + d, inner)

        def peer_h(d):
            return lax.rem(hd + d, n_head)

        for d in range(1, inner):
            greet(peer_x(d), hd)
        for d in range(1, n_head):
            greet(me, peer_h(d))

        @pl.when(me > 0)
        def _():
            greet(me - 1, hd)

        @pl.when(me < n_seq - 1)
        def _():
            greet(me + 1, hd)

        @pl.when(z > 0)
        def _():
            greet(me - inner, hd)

        @pl.when(z < outer - 1)
        def _():
            greet(me + inner, hd)

        @pl.when(me == 0)
        def _():
            left[...] = jnp.zeros(left.shape, BF16)

        @pl.when(me == n_seq - 1)
        def _():
            hrecv[...] = jnp.zeros(hrecv.shape, BF16)

        @pl.when(z == 0)
        def _():
            zrecv[0] = jnp.zeros(zrecv.shape[1:], BF16)

        @pl.when(z == outer - 1)
        def _():
            zrecv[1] = jnp.zeros(zrecv.shape[1:], BF16)

        xs[:, 0:RIM, :] = jnp.zeros((3, RIM, HEAD_DIM), F32)
        s_acc[...] = jnp.zeros(s_acc.shape, F32)
        i_acc[...] = jnp.zeros(i_acc.shape, F32)

        guests = inner - 1 + n_head - 1
        for there in (me > 0, me < n_seq - 1, z > 0, z < outer - 1):
            guests = guests + there.astype(jnp.int32)
        pl.semaphore_wait(bar, guests)

        left_copy = pltpu.make_async_remote_copy(
            src_ref=x_hbm.at[:, rows - RIM : rows, :],
            dst_ref=left,
            send_sem=lsem.at[0],
            recv_sem=lsem.at[1],
            device_id=(lax.rem(me + 1, n_seq), hd),
            device_id_type=MESH,
        )

        @pl.when(me < n_seq - 1)
        def _():
            left_copy.start()

        def conv_rows(i, h, count):
            total = w_ref[i, 0:1, col(h)] * xs[i, RIM : RIM + count, :]
            for j in range(1, taps):
                total = total + w_ref[i, j : j + 1, col(h)] * xs[i, RIM - j : RIM - j + count, :]
            return total.astype(BF16)

        @pl.loop(0, heads)
        def _(h):
            in_copy(h).wait()
            for i in range(3):
                xs[i, RIM : RIM + rows, :] = xin[i, :, col(h)].astype(F32)
                qkv[i, h] = conv_rows(i, h, rows)

        @pl.when(me > 0)
        def _():
            left_copy.wait_recv()

        def x_copy(way, d, h):
            return pltpu.make_async_remote_copy(
                src_ref=xsend.at[way, h],
                dst_ref=xrecv.at[way, d - 1, h],
                send_sem=xsem_s.at[way, d - 1, h],
                recv_sem=xsem_r.at[way, d - 1, h],
                device_id=(peer_x(d), hd),
                device_id_type=MESH,
            )

        def z_copy(way, h):
            target = jnp.minimum(z + 1, outer - 1) if way == 0 else jnp.maximum(z - 1, 0)
            return pltpu.make_async_remote_copy(
                src_ref=zsend.at[way, h],
                dst_ref=zrecv.at[way, h],
                send_sem=zsem_s.at[way, h],
                recv_sem=zsem_r.at[way, h],
                device_id=(target * inner + x, hd),
                device_id_type=MESH,
            )

        has_prev = (z > 0, z < outer - 1)
        has_next = (z < outer - 1, z > 0)

        def scan_step(way, h):
            part = jnp.zeros((HEAD_DIM, HEAD_DIM), F32)
            total = own[h]
            for d in range(1, inner):
                x_copy(way, d, h).wait_recv()
                got = xrecv[way, d - 1, h].astype(F32)
                total = total + got
                before = (x >= d) if way == 0 else (x < d)
                part = part + got * before.astype(F32)

            @pl.when(has_prev[way])
            def _():
                z_copy(way, h).wait_recv()

            entering = zrecv[way, h].astype(F32)

            @pl.when(has_next[way])
            def _():
                zsend[way, h] = (entering + total).astype(BF16)
                z_copy(way, h).start()

            stb[way, h] = (entering + part).astype(BF16)

        def share(way, h, state):
            own[h] = state
            xsend[way, h] = state.astype(BF16)
            for d in range(1, inner):
                x_copy(way, d, h).start()

        @pl.loop(0, heads)
        def _(h):
            for i in range(3):
                xs[i, 0:RIM, :] = left[i, :, col(h)].astype(F32)
                xs[i, RIM : RIM + TAIL, :] = xin[i, 0:TAIL, col(h)].astype(F32)
                qkv[i, h, 0:TAIL, :] = conv_rows(i, h, TAIL)
            share(0, h, dot(qkv[1, h], qkv[2, h], 0, 0))

        lag = (jnp.minimum(2 + 2 * z, heads), jnp.minimum(2 + 2 * (outer - 1 - z), heads))
        low0 = lower_mask(half, half, 0)
        low1 = lower_mask(half, rows, half)
        up0 = upper_mask(half, rows)
        up1 = upper_mask(half, half)

        @pl.loop(0, heads)
        def _(h):
            q0, q1 = qkv[0, h, 0:half, :], qkv[0, h, half:rows, :]
            k0, k1 = qkv[1, h, 0:half, :], qkv[1, h, half:rows, :]
            k, v, q = qkv[1, h], qkv[2, h], qkv[0, h]
            sc = jnp.where(low0, dot(q0, k0, 1, 1), 0.0).astype(BF16)
            att[h, 0:half, :] = dot(sc, v[0:half], 1, 0)
            sc = jnp.where(low1, dot(q1, k, 1, 1), 0.0).astype(BF16)
            att[h, half:rows, :] = dot(sc, v, 1, 0)
            scT[h, 0:half, :] = jnp.where(up0, dot(k0, q, 1, 1), 0.0).astype(BF16)
            scT[h, half:rows, half:rows] = jnp.where(up1, dot(k1, q1, 1, 1), 0.0).astype(BF16)

            @pl.when(h >= lag[0])
            def _():
                scan_step(0, h - lag[0])

        c_copy.wait()

        @pl.loop(0, heads)
        def _(h):
            @pl.when(h >= heads - lag[0])
            def _():
                scan_step(0, h)

            a = dot(qkv[0, h], stb[0, h], 1, 0) + att[h]
            att[h] = a
            s_acc[...] += a * a
            i_acc[...] += (gain_ref[:, col(h)] * cin[:, col(h)].astype(F32)) * a

        sums = []
        for acc in (s_acc, i_acc):
            for b in range(groups):
                piece = acc[b * HEAD_DIM : (b + 1) * HEAD_DIM, :].T
                sums.append(jnp.sum(piece, axis=0, keepdims=True))
        stat_s[...] = jnp.concatenate(sums, axis=0)

        def s_copy(d):
            return pltpu.make_async_remote_copy(
                src_ref=stat_s,
                dst_ref=stat_r.at[d - 1],
                send_sem=ssem_s.at[d - 1],
                recv_sem=ssem_r.at[d - 1],
                device_id=(me, peer_h(d)),
                device_id_type=MESH,
            )

        for d in range(1, n_head):
            s_copy(d).start()
        stats = stat_s[...]
        for d in range(1, n_head):
            s_copy(d).wait_recv()
            stats = stats + stat_r[d - 1]
        rms = jnp.sqrt(stats[0:groups] / width + 1e-05)
        inv = 1.0 / rms
        coef = stats[groups : 2 * groups] / (width * rms * rms * rms)
        turned = jnp.concatenate([inv, coef], axis=0).T
        for b in range(groups):
            at = slice(b * HEAD_DIM, (b + 1) * HEAD_DIM)
            rb[at, :] = jnp.broadcast_to(turned[:, b : b + 1], (HEAD_DIM, HEAD_DIM))
            cb[at, :] = jnp.broadcast_to(
                turned[:, groups + b : groups + b + 1], (HEAD_DIM, HEAD_DIM)
            )

        @pl.loop(0, heads)
        def _(h):
            weighted = gain_ref[:, col(h)] * cin[:, col(h)].astype(F32)
            g = (weighted * rb[...] - att[h] * cb[...]).astype(BF16)
            gb[h] = g
            share(1, h, dot(qkv[0, h], g, 0, 0))

        def out_copy(h):
            return pltpu.make_async_copy(outb.at[:, col(h)], out_hbm.at[:, col(h)], out_sem.at[h])

        @pl.loop(0, heads)
        def _(h):
            outb[:, col(h)] = (gain_ref[:, col(h)] * att[h] * rb[...]).astype(BF16)
            out_copy(h).start()
            g, q, k, v = gb[h], qkv[0, h], qkv[1, h], qkv[2, h]
            across = dot(g, stb[0, h], 1, 1)
            m = jnp.where(low0, dot(g[0:half], v[0:half], 1, 1), 0.0).astype(BF16)
            gq[h, 0:half, :] = (across[0:half] + dot(m, k[0:half], 1, 0)).astype(BF16)
            m = jnp.where(low1, dot(g[half:rows], v, 1, 1), 0.0).astype(BF16)
            gq[h, half:rows, :] = (across[half:rows] + dot(m, k, 1, 0)).astype(BF16)
            m = jnp.where(up0, dot(v[0:half], g, 1, 1), 0.0).astype(BF16)
            gkv[0, h, 0:half, :] = dot(m, q, 1, 0)
            m = jnp.where(up1, dot(v[half:rows], g[half:rows], 1, 1), 0.0).astype(BF16)
            gkv[0, h, half:rows, :] = dot(m, q[half:rows], 1, 0)
            gkv[1, h, 0:half, :] = dot(scT[h, 0:half, :], g, 1, 0)
            gkv[1, h, half:rows, :] = dot(scT[h, half:rows, half:rows], g[half:rows], 1, 0)

            @pl.when(h >= lag[1])
            def _():
                scan_step(1, h - lag[1])

        def h_copy(h):
            return pltpu.make_async_remote_copy(
                src_ref=hsend.at[h],
                dst_ref=hrecv.at[h],
                send_sem=hsem_s.at[h],
                recv_sem=hsem_r.at[h],
                device_id=(jnp.maximum(me - 1, 0), hd),
                device_id_type=MESH,
            )

        body_rows = rows - TAIL

        def gi_copy(h):
            return pltpu.make_async_copy(
                gib.at[:, 0:body_rows, col(h)], gi_hbm.at[:, 0:body_rows, col(h)], gi_sem.at[h]
            )

        def back_rows(i, h, read, count):
            total = w_ref[i, 0:1, col(h)] * read(0, count)
            for j in range(1, taps):
                total = total + w_ref[i, j : j + 1, col(h)] * read(j, count)
            return total.astype(BF16)

        @pl.loop(0, heads)
        def _(h):
            @pl.when(h >= heads - lag[1])
            def _():
                scan_step(1, h)

            after = stb[1, h]
            gk = (gkv[0, h] + dot(qkv[2, h], after, 1, 1)).astype(BF16)
            gv = (gkv[1, h] + dot(qkv[1, h], after, 1, 0)).astype(BF16)
            for i, grad in enumerate((gq[h], gk, gv)):
                full = grad.astype(F32)
                xs[i, 0:rows, :] = full
                hsend[h, i] = xs[i, 0:RIM, :].astype(BF16)
                tail[h, i, 0:TAIL, :] = xs[i, rows - TAIL : rows, :]

            @pl.when(me > 0)
            def _():
                h_copy(h).start()

            for i in range(3):
                gib[i, 0:body_rows, col(h)] = back_rows(
                    i, h, lambda j, count, i=i: xs[i, j : j + count, :], body_rows
                )
            gi_copy(h).start()

        @pl.loop(0, heads)
        def _(h):
            @pl.when(me < n_seq - 1)
            def _():
                h_copy(h).wait_recv()

            for i in range(3):
                tail[h, i, TAIL : TAIL + RIM, :] = hrecv[h, i].astype(F32)
                gib[i, body_rows:rows, col(h)] = back_rows(
                    i, h, lambda j, count, i=i: tail[h, i, j : j + count, :], TAIL
                )

        tail_copy = pltpu.make_async_copy(
            gib.at[:, body_rows:rows, :], gi_hbm.at[:, body_rows:rows, :], tail_sem
        )
        tail_copy.start()

        @pl.when(me < n_seq - 1)
        def _():
            left_copy.wait_send()

        for d in range(1, n_head):
            s_copy(d).wait_send()

        @pl.loop(0, heads)
        def _(h):
            out_copy(h).wait()
            gi_copy(h).wait()
            for way in range(2):
                for d in range(1, inner):
                    x_copy(way, d, h).wait_send()

                @pl.when(has_next[way])
                def _():
                    z_copy(way, h).wait_send()

            @pl.when(me > 0)
            def _():
                h_copy(h).wait_send()

        tail_copy.wait()

    dma = pltpu.SemaphoreType.DMA
    state = (heads, HEAD_DIM, HEAD_DIM)
    scratch = [
        pltpu.VMEM((3, rows, cols), BF16),
        pltpu.VMEM((rows, cols), BF16),
        pltpu.VMEM((3, heads, rows, HEAD_DIM), BF16),
        pltpu.VMEM((3, rows + RIM, HEAD_DIM), F32),
        pltpu.VMEM((3, RIM, cols), BF16),
        pltpu.VMEM((heads, rows, rows), BF16),
        pltpu.VMEM((heads, rows, HEAD_DIM), F32),
        pltpu.VMEM((2,) + state, BF16),
        pltpu.VMEM((rows, HEAD_DIM), F32),
        pltpu.VMEM((rows, HEAD_DIM), F32),
        pltpu.VMEM((2 * groups, HEAD_DIM), F32),
        pltpu.VMEM((n_head - 1, 2 * groups, HEAD_DIM), F32),
        pltpu.VMEM((rows, HEAD_DIM), F32),
        pltpu.VMEM((rows, HEAD_DIM), F32),
        pltpu.VMEM((heads, rows, HEAD_DIM), BF16),
        pltpu.VMEM((rows, cols), BF16),
        pltpu.VMEM((heads, rows, HEAD_DIM), BF16),
        pltpu.VMEM((2, heads, rows, HEAD_DIM), F32),
        pltpu.VMEM((heads, 3, TAIL + RIM, HEAD_DIM), F32),
        pltpu.VMEM((3, rows, cols), BF16),
        pltpu.VMEM(state, F32),
        pltpu.VMEM((2,) + state, BF16),
        pltpu.VMEM((2, inner - 1) + state, BF16),
        pltpu.VMEM((2,) + state, BF16),
        pltpu.VMEM((2,) + state, BF16),
        pltpu.VMEM((heads, 3, RIM, HEAD_DIM), BF16),
        pltpu.VMEM((heads, 3, RIM, HEAD_DIM), BF16),
        dma((heads,)),
        dma,
        dma((heads,)),
        dma((heads,)),
        dma,
        dma((2,)),
        dma((2, inner - 1, heads)),
        dma((2, inner - 1, heads)),
        dma((2, heads)),
        dma((2, heads)),
        dma((n_head - 1,)),
        dma((n_head - 1,)),
        dma((heads,)),
        dma((heads,)),
    ]
    return kernel, scratch


def solution(mesh):
    n_seq, n_head = mesh.shape["seq"], mesh.shape["head"]

    def body(inputs, conv_weight, gain, cotangent):
        _, rows, cols = inputs.shape
        assert rows == BLOCK and n_seq > 1 and n_head > 1
        kernel, scratch = make_kernel(n_seq, n_head, rows, cols, conv_weight.shape[1])
        hbm = pl.BlockSpec(memory_space=pl.ANY)
        vmem = pl.BlockSpec(memory_space=pltpu.VMEM)
        return pl.pallas_call(
            kernel,
            out_shape=(
                jax.ShapeDtypeStruct((rows, cols), BF16),
                jax.ShapeDtypeStruct((3, rows, cols), BF16),
            ),
            in_specs=[hbm, vmem, vmem, hbm],
            out_specs=(hbm, hbm),
            scratch_shapes=scratch,
            compiler_params=pltpu.CompilerParams(
                collective_id=0, has_side_effects=True, vmem_limit_bytes=56 * 1024 * 1024
            ),
            name="block",
        )(inputs, conv_weight, gain.reshape(1, cols), cotangent)

    placed = (P(None, "seq", "head"), P(None, None, "head"), P("head"), P("seq", "head"))
    return jax.shard_map(
        body,
        mesh=mesh,
        in_specs=placed,
        out_specs=(P("seq", "head"), P(None, "seq", "head")),
        check_vma=False,
    )
```

```python
import jax
import jax.numpy as jnp
from jax import lax
from jax.experimental import pallas as pl
from jax.experimental.pallas import tpu as pltpu
from jax.sharding import PartitionSpec as P

HEAD_DIM = 128
BLOCK = 512
RIM = 8
TAIL = 16
F32 = jnp.float32
BF16 = jnp.bfloat16
MESH = pl.DeviceIdType.MESH


def dot(a, b, ca, cb):
    return lax.dot_general(a, b, (((ca,), (cb,)), ((), ())), preferred_element_type=F32)


def split_of(count):
    inner = 1
    while inner * inner * 4 <= count and count % (inner * 2) == 0:
        inner *= 2
    return count // inner, inner


def lower_mask(rows, cols, shift):
    return lax.broadcasted_iota(jnp.int32, (rows, cols), 0) + shift >= lax.broadcasted_iota(
        jnp.int32, (rows, cols), 1
    )


def upper_mask(rows, cols):
    return lax.broadcasted_iota(jnp.int32, (rows, cols), 0) <= lax.broadcasted_iota(
        jnp.int32, (rows, cols), 1
    )


def make_kernel(n_seq, n_head, rows, cols, taps):
    outer, inner = split_of(n_seq)
    heads = cols // HEAD_DIM
    width = cols * n_head
    half = rows // 2
    groups = rows // HEAD_DIM

    def kernel(
        x_hbm, w_ref, gain_ref, c_hbm, out_hbm, gi_hbm,
        xin, cin, qkv, xs, left, scT, att, stb, s_acc, i_acc,
        stat_s, stat_r, rb, cb, gb, outb, gq, gkv, tail, gib,
        own, xsend, xrecv, zsend, zrecv, hsend, hrecv,
        in_sem, c_sem, out_sem, gi_sem, tail_sem, lsem, xsem_s, xsem_r, zsem_s, zsem_r,
        ssem_s, ssem_r, hsem_s, hsem_r,
    ):
        me = lax.axis_index("seq")
        hd = lax.axis_index("head")
        z = me // inner
        x = lax.rem(me, inner)

        def col(h):
            return pl.ds(pl.multiple_of(h * HEAD_DIM, HEAD_DIM), HEAD_DIM)

        def in_copy(h):
            return pltpu.make_async_copy(
                x_hbm.at[:, :, col(h)], xin.at[:, :, col(h)], in_sem.at[h]
            )

        c_copy = pltpu.make_async_copy(c_hbm, cin, c_sem)

        bar = pltpu.get_barrier_semaphore()

        def greet(seq, head):
            pl.semaphore_signal(bar, inc=1, device_id=(seq, head), device_id_type=MESH)

        def peer_x(d):
            return z * inner + lax.rem(x + d, inner)

        def peer_h(d):
            return lax.rem(hd + d, n_head)

        for d in range(1, inner):
            greet(peer_x(d), hd)
        for d in range(1, n_head):
            greet(me, peer_h(d))

        @pl.when(me > 0)
        def _():
            greet(me - 1, hd)

        @pl.when(me < n_seq - 1)
        def _():
            greet(me + 1, hd)

        @pl.when(z > 0)
        def _():
            greet(me - inner, hd)

        @pl.when(z < outer - 1)
        def _():
            greet(me + inner, hd)

        @pl.loop(0, heads)
        def _(h):
            in_copy(h).start()

        c_copy.start()

        @pl.when(me == 0)
        def _():
            left[...] = jnp.zeros(left.shape, BF16)

        @pl.when(me == n_seq - 1)
        def _():
            hrecv[...] = jnp.zeros(hrecv.shape, BF16)

        @pl.when(z == 0)
        def _():
            zrecv[0] = jnp.zeros(zrecv.shape[1:], BF16)

        @pl.when(z == outer - 1)
        def _():
            zrecv[1] = jnp.zeros(zrecv.shape[1:], BF16)

        xs[:, 0:RIM, :] = jnp.zeros((3, RIM, HEAD_DIM), F32)
        s_acc[...] = jnp.zeros(s_acc.shape, F32)
        i_acc[...] = jnp.zeros(i_acc.shape, F32)

        guests = inner - 1 + n_head - 1
        for there in (me > 0, me < n_seq - 1, z > 0, z < outer - 1):
            guests = guests + there.astype(jnp.int32)
        pl.semaphore_wait(bar, guests)

        left_copy = pltpu.make_async_remote_copy(
            src_ref=x_hbm.at[:, rows - RIM : rows, :],
            dst_ref=left,
            send_sem=lsem.at[0],
            recv_sem=lsem.at[1],
            device_id=(lax.rem(me + 1, n_seq), hd),
            device_id_type=MESH,
        )

        @pl.when(me < n_seq - 1)
        def _():
            left_copy.start()

        def conv_rows(i, h, count):
            total = w_ref[i, 0:1, col(h)] * xs[i, RIM : RIM + count, :]
            for j in range(1, taps):
                total = total + w_ref[i, j : j + 1, col(h)] * xs[i, RIM - j : RIM - j + count, :]
            return total.astype(BF16)

        @pl.loop(0, heads)
        def _(h):
            in_copy(h).wait()
            for i in (1, 2):
                xs[i, RIM : RIM + rows, :] = xin[i, :, col(h)].astype(F32)
                qkv[i, h] = conv_rows(i, h, rows)

        @pl.when(me > 0)
        def _():
            left_copy.wait_recv()

        def x_copy(way, d, h):
            return pltpu.make_async_remote_copy(
                src_ref=xsend.at[way, h],
                dst_ref=xrecv.at[way, d - 1, h],
                send_sem=xsem_s.at[way, d - 1, h],
                recv_sem=xsem_r.at[way, d - 1, h],
                device_id=(peer_x(d), hd),
                device_id_type=MESH,
            )

        def z_copy(way, h):
            target = jnp.minimum(z + 1, outer - 1) if way == 0 else jnp.maximum(z - 1, 0)
            return pltpu.make_async_remote_copy(
                src_ref=zsend.at[way, h],
                dst_ref=zrecv.at[way, h],
                send_sem=zsem_s.at[way, h],
                recv_sem=zsem_r.at[way, h],
                device_id=(target * inner + x, hd),
                device_id_type=MESH,
            )

        has_prev = (z > 0, z < outer - 1)
        has_next = (z < outer - 1, z > 0)

        def scan_step(way, h):
            part = jnp.zeros((HEAD_DIM, HEAD_DIM), F32)
            total = own[h]
            for d in range(1, inner):
                x_copy(way, d, h).wait_recv()
                got = xrecv[way, d - 1, h].astype(F32)
                total = total + got
                before = (x >= d) if way == 0 else (x < d)
                part = part + got * before.astype(F32)

            @pl.when(has_prev[way])
            def _():
                z_copy(way, h).wait_recv()

            entering = zrecv[way, h].astype(F32)

            @pl.when(has_next[way])
            def _():
                zsend[way, h] = (entering + total).astype(BF16)
                z_copy(way, h).start()

            stb[way, h] = (entering + part).astype(BF16)

        def share(way, h, state):
            own[h] = state
            xsend[way, h] = state.astype(BF16)
            for d in range(1, inner):
                x_copy(way, d, h).start()

        @pl.loop(0, heads)
        def _(h):
            for i in (1, 2):
                xs[i, 0:RIM, :] = left[i, :, col(h)].astype(F32)
                xs[i, RIM : RIM + TAIL, :] = xin[i, 0:TAIL, col(h)].astype(F32)
                qkv[i, h, 0:TAIL, :] = conv_rows(i, h, TAIL)
            share(0, h, dot(qkv[1, h], qkv[2, h], 0, 0))

        lag = (jnp.minimum(2 + 3 * z, heads), jnp.minimum(1 + 3 * (outer - 1 - z), heads))
        low0 = lower_mask(half, half, 0)
        low1 = lower_mask(half, rows, half)
        up0 = upper_mask(half, rows)
        up1 = upper_mask(half, half)

        @pl.loop(0, heads)
        def _(h):
            xs[0, 0:RIM, :] = left[0, :, col(h)].astype(F32)
            xs[0, RIM : RIM + rows, :] = xin[0, :, col(h)].astype(F32)
            qkv[0, h] = conv_rows(0, h, rows)
            q0, q1 = qkv[0, h, 0:half, :], qkv[0, h, half:rows, :]
            k0, k1 = qkv[1, h, 0:half, :], qkv[1, h, half:rows, :]
            k, v, q = qkv[1, h], qkv[2, h], qkv[0, h]
            sc = jnp.where(low0, dot(q0, k0, 1, 1), 0.0).astype(BF16)
            att[h, 0:half, :] = dot(sc, v[0:half], 1, 0)
            sc = jnp.where(low1, dot(q1, k, 1, 1), 0.0).astype(BF16)
            att[h, half:rows, :] = dot(sc, v, 1, 0)
            scT[h, 0:half, :] = jnp.where(up0, dot(k0, q, 1, 1), 0.0).astype(BF16)
            scT[h, half:rows, half:rows] = jnp.where(up1, dot(k1, q1, 1, 1), 0.0).astype(BF16)

            @pl.when(h >= lag[0])
            def _():
                scan_step(0, h - lag[0])

        c_copy.wait()

        @pl.loop(0, heads)
        def _(h):
            @pl.when(h >= heads - lag[0])
            def _():
                scan_step(0, h)

            a = dot(qkv[0, h], stb[0, h], 1, 0) + att[h]
            att[h] = a
            s_acc[...] += a * a
            i_acc[...] += (gain_ref[:, col(h)] * cin[:, col(h)].astype(F32)) * a

        sums = []
        for acc in (s_acc, i_acc):
            for b in range(groups):
                piece = acc[b * HEAD_DIM : (b + 1) * HEAD_DIM, :].T
                sums.append(jnp.sum(piece, axis=0, keepdims=True))
        stat_s[...] = jnp.concatenate(sums, axis=0)

        def s_copy(d):
            return pltpu.make_async_remote_copy(
                src_ref=stat_s,
                dst_ref=stat_r.at[d - 1],
                send_sem=ssem_s.at[d - 1],
                recv_sem=ssem_r.at[d - 1],
                device_id=(me, peer_h(d)),
                device_id_type=MESH,
            )

        for d in range(1, n_head):
            s_copy(d).start()
        stats = stat_s[...]
        for d in range(1, n_head):
            s_copy(d).wait_recv()
            stats = stats + stat_r[d - 1]
        rms = jnp.sqrt(stats[0:groups] / width + 1e-05)
        inv = 1.0 / rms
        coef = stats[groups : 2 * groups] / (width * rms * rms * rms)
        turned = jnp.concatenate([inv, coef], axis=0).T
        for b in range(groups):
            at = slice(b * HEAD_DIM, (b + 1) * HEAD_DIM)
            rb[at, :] = jnp.broadcast_to(turned[:, b : b + 1], (HEAD_DIM, HEAD_DIM))
            cb[at, :] = jnp.broadcast_to(
                turned[:, groups + b : groups + b + 1], (HEAD_DIM, HEAD_DIM)
            )

        @pl.loop(0, heads)
        def _(h):
            weighted = gain_ref[:, col(h)] * cin[:, col(h)].astype(F32)
            g = (weighted * rb[...] - att[h] * cb[...]).astype(BF16)
            gb[h] = g
            share(1, h, dot(qkv[0, h], g, 0, 0))

        def out_copy(h):
            return pltpu.make_async_copy(outb.at[:, col(h)], out_hbm.at[:, col(h)], out_sem.at[h])

        @pl.loop(0, heads)
        def _(h):
            outb[:, col(h)] = (gain_ref[:, col(h)] * att[h] * rb[...]).astype(BF16)
            out_copy(h).start()
            g, q, k, v = gb[h], qkv[0, h], qkv[1, h], qkv[2, h]
            across = dot(g, stb[0, h], 1, 1)
            m = jnp.where(low0, dot(g[0:half], v[0:half], 1, 1), 0.0).astype(BF16)
            gq[h, 0:half, :] = (across[0:half] + dot(m, k[0:half], 1, 0)).astype(BF16)
            m = jnp.where(low1, dot(g[half:rows], v, 1, 1), 0.0).astype(BF16)
            gq[h, half:rows, :] = (across[half:rows] + dot(m, k, 1, 0)).astype(BF16)
            m = jnp.where(up0, dot(v[0:half], g, 1, 1), 0.0).astype(BF16)
            gkv[0, h, 0:half, :] = dot(m, q, 1, 0)
            m = jnp.where(up1, dot(v[half:rows], g[half:rows], 1, 1), 0.0).astype(BF16)
            gkv[0, h, half:rows, :] = dot(m, q[half:rows], 1, 0)
            gkv[1, h, 0:half, :] = dot(scT[h, 0:half, :], g, 1, 0)
            gkv[1, h, half:rows, :] = dot(scT[h, half:rows, half:rows], g[half:rows], 1, 0)

            @pl.when(h >= lag[1])
            def _():
                scan_step(1, h - lag[1])

        def h_copy(h):
            return pltpu.make_async_remote_copy(
                src_ref=hsend.at[h],
                dst_ref=hrecv.at[h],
                send_sem=hsem_s.at[h],
                recv_sem=hsem_r.at[h],
                device_id=(jnp.maximum(me - 1, 0), hd),
                device_id_type=MESH,
            )

        body_rows = rows - TAIL

        def gi_copy(h):
            return pltpu.make_async_copy(
                gib.at[:, 0:body_rows, col(h)], gi_hbm.at[:, 0:body_rows, col(h)], gi_sem.at[h]
            )

        def back_rows(i, h, read, count):
            total = w_ref[i, 0:1, col(h)] * read(0, count)
            for j in range(1, taps):
                total = total + w_ref[i, j : j + 1, col(h)] * read(j, count)
            return total.astype(BF16)

        @pl.loop(0, heads)
        def _(h):
            @pl.when(h >= heads - lag[1])
            def _():
                scan_step(1, h)

            after = stb[1, h]
            gk = (gkv[0, h] + dot(qkv[2, h], after, 1, 1)).astype(BF16)
            gv = (gkv[1, h] + dot(qkv[1, h], after, 1, 0)).astype(BF16)
            for i, grad in enumerate((gq[h], gk, gv)):
                full = grad.astype(F32)
                xs[i, 0:rows, :] = full
                hsend[h, i] = xs[i, 0:RIM, :].astype(BF16)
                tail[h, i, 0:TAIL, :] = xs[i, rows - TAIL : rows, :]

            @pl.when(me > 0)
            def _():
                h_copy(h).start()

            for i in range(3):
                gib[i, 0:body_rows, col(h)] = back_rows(
                    i, h, lambda j, count, i=i: xs[i, j : j + count, :], body_rows
                )
            gi_copy(h).start()

        @pl.loop(0, heads)
        def _(h):
            @pl.when(me < n_seq - 1)
            def _():
                h_copy(h).wait_recv()

            for i in range(3):
                tail[h, i, TAIL : TAIL + RIM, :] = hrecv[h, i].astype(F32)
                gib[i, body_rows:rows, col(h)] = back_rows(
                    i, h, lambda j, count, i=i: tail[h, i, j : j + count, :], TAIL
                )

        tail_copy = pltpu.make_async_copy(
            gib.at[:, body_rows:rows, :], gi_hbm.at[:, body_rows:rows, :], tail_sem
        )
        tail_copy.start()

        @pl.when(me < n_seq - 1)
        def _():
            left_copy.wait_send()

        for d in range(1, n_head):
            s_copy(d).wait_send()

        @pl.loop(0, heads)
        def _(h):
            out_copy(h).wait()
            gi_copy(h).wait()
            for way in range(2):
                for d in range(1, inner):
                    x_copy(way, d, h).wait_send()

                @pl.when(has_next[way])
                def _():
                    z_copy(way, h).wait_send()

            @pl.when(me > 0)
            def _():
                h_copy(h).wait_send()

        tail_copy.wait()

    dma = pltpu.SemaphoreType.DMA
    state = (heads, HEAD_DIM, HEAD_DIM)
    scratch = [
        pltpu.VMEM((3, rows, cols), BF16),
        pltpu.VMEM((rows, cols), BF16),
        pltpu.VMEM((3, heads, rows, HEAD_DIM), BF16),
        pltpu.VMEM((3, rows + RIM, HEAD_DIM), F32),
        pltpu.VMEM((3, RIM, cols), BF16),
        pltpu.VMEM((heads, rows, rows), BF16),
        pltpu.VMEM((heads, rows, HEAD_DIM), F32),
        pltpu.VMEM((2,) + state, BF16),
        pltpu.VMEM((rows, HEAD_DIM), F32),
        pltpu.VMEM((rows, HEAD_DIM), F32),
        pltpu.VMEM((2 * groups, HEAD_DIM), F32),
        pltpu.VMEM((n_head - 1, 2 * groups, HEAD_DIM), F32),
        pltpu.VMEM((rows, HEAD_DIM), F32),
        pltpu.VMEM((rows, HEAD_DIM), F32),
        pltpu.VMEM((heads, rows, HEAD_DIM), BF16),
        pltpu.VMEM((rows, cols), BF16),
        pltpu.VMEM((heads, rows, HEAD_DIM), BF16),
        pltpu.VMEM((2, heads, rows, HEAD_DIM), F32),
        pltpu.VMEM((heads, 3, TAIL + RIM, HEAD_DIM), F32),
        pltpu.VMEM((3, rows, cols), BF16),
        pltpu.VMEM(state, F32),
        pltpu.VMEM((2,) + state, BF16),
        pltpu.VMEM((2, inner - 1) + state, BF16),
        pltpu.VMEM((2,) + state, BF16),
        pltpu.VMEM((2,) + state, BF16),
        pltpu.VMEM((heads, 3, RIM, HEAD_DIM), BF16),
        pltpu.VMEM((heads, 3, RIM, HEAD_DIM), BF16),
        dma((heads,)),
        dma,
        dma((heads,)),
        dma((heads,)),
        dma,
        dma((2,)),
        dma((2, inner - 1, heads)),
        dma((2, inner - 1, heads)),
        dma((2, heads)),
        dma((2, heads)),
        dma((n_head - 1,)),
        dma((n_head - 1,)),
        dma((heads,)),
        dma((heads,)),
    ]
    return kernel, scratch


def place(output, grads, output_hbm, grads_hbm, sem):
    copies = [pltpu.make_async_copy(output, output_hbm, sem.at[3])]
    for i in range(3):
        copies.append(pltpu.make_async_copy(grads.at[i], grads_hbm.at[i], sem.at[i]))
    for copy in copies:
        copy.start()
    for copy in copies:
        copy.wait()


def solution(mesh):
    n_seq, n_head = mesh.shape["seq"], mesh.shape["head"]

    def body(inputs, conv_weight, gain, cotangent):
        _, rows, cols = inputs.shape
        assert rows == BLOCK and n_seq > 1 and n_head > 1
        kernel, scratch = make_kernel(n_seq, n_head, rows, cols, conv_weight.shape[1])
        anywhere = pl.BlockSpec(memory_space=pl.ANY)
        hbm = pl.BlockSpec(memory_space=pltpu.HBM)
        vmem = pl.BlockSpec(memory_space=pltpu.VMEM)
        shapes = (
            jax.ShapeDtypeStruct((rows, cols), BF16),
            jax.ShapeDtypeStruct((3, rows, cols), BF16),
        )
        output, grads = pl.pallas_call(
            kernel,
            out_shape=(pltpu.VMEM((rows, cols), BF16), pltpu.VMEM((3, rows, cols), BF16)),
            in_specs=[hbm, vmem, vmem, hbm],
            out_specs=(anywhere, anywhere),
            scratch_shapes=scratch,
            compiler_params=pltpu.CompilerParams(
                collective_id=0, has_side_effects=True, vmem_limit_bytes=58 * 1024 * 1024
            ),
            name="block",
        )(inputs, conv_weight, gain.reshape(1, cols), cotangent)
        return pl.pallas_call(
            place,
            out_shape=shapes,
            in_specs=[anywhere, anywhere],
            out_specs=(hbm, hbm),
            scratch_shapes=[pltpu.SemaphoreType.DMA((4,))],
            compiler_params=pltpu.CompilerParams(vmem_limit_bytes=1024 * 1024),
            name="place",
        )(output, grads)

    placed = (P(None, "seq", "head"), P(None, None, "head"), P("head"), P("seq", "head"))
    return jax.shard_map(
        body,
        mesh=mesh,
        in_specs=placed,
        out_specs=(P("seq", "head"), P(None, "seq", "head")),
        check_vma=False,
    )
```

```python
import jax
import jax.numpy as jnp
from jax import lax
from jax.experimental import pallas as pl
from jax.experimental.pallas import tpu as pltpu
from jax.sharding import PartitionSpec as P

HEAD_DIM = 128
BLOCK = 512
RIM = 8
TAIL = 16
F32 = jnp.float32
BF16 = jnp.bfloat16
MESH = pl.DeviceIdType.MESH


def dot(a, b, ca, cb):
    return lax.dot_general(a, b, (((ca,), (cb,)), ((), ())), preferred_element_type=F32)


def split_of(count):
    inner = 1
    while inner * inner * 4 <= count and count % (inner * 2) == 0:
        inner *= 2
    return count // inner, inner


def lower_mask(rows, cols, shift):
    return lax.broadcasted_iota(jnp.int32, (rows, cols), 0) + shift >= lax.broadcasted_iota(
        jnp.int32, (rows, cols), 1
    )


def upper_mask(rows, cols):
    return lax.broadcasted_iota(jnp.int32, (rows, cols), 0) <= lax.broadcasted_iota(
        jnp.int32, (rows, cols), 1
    )


def make_kernel(n_seq, n_head, rows, cols, taps):
    outer, inner = split_of(n_seq)
    heads = cols // HEAD_DIM
    width = cols * n_head
    half = rows // 2
    groups = rows // HEAD_DIM

    def kernel(
        x_hbm, w_ref, gain_ref, c_hbm, out_hbm, gi_hbm,
        xin, cin, qkv, xs, left, scT, att, stb, s_acc, i_acc,
        stat_s, stat_r, rb, cb, gb, outb, gq, gkv, tail, gib,
        own, xsend, xrecv, zsend, zrecv, hsend, hrecv,
        in_sem, c_sem, out_sem, gi_sem, tail_sem, lsem, xsem_s, xsem_r, zsem_s, zsem_r,
        ssem_s, ssem_r, hsem_s, hsem_r,
    ):
        me = lax.axis_index("seq")
        hd = lax.axis_index("head")
        z = me // inner
        x = lax.rem(me, inner)

        def col(h):
            return pl.ds(pl.multiple_of(h * HEAD_DIM, HEAD_DIM), HEAD_DIM)

        def in_copy(h):
            return pltpu.make_async_copy(
                x_hbm.at[:, :, col(h)], xin.at[:, :, col(h)], in_sem.at[h]
            )

        c_copy = pltpu.make_async_copy(c_hbm, cin, c_sem)

        bar = pltpu.get_barrier_semaphore()

        def greet(seq, head):
            pl.semaphore_signal(bar, inc=1, device_id=(seq, head), device_id_type=MESH)

        def peer_x(d):
            return z * inner + lax.rem(x + d, inner)

        def peer_h(d):
            return lax.rem(hd + d, n_head)

        for d in range(1, inner):
            greet(peer_x(d), hd)
        for d in range(1, n_head):
            greet(me, peer_h(d))

        @pl.when(me > 0)
        def _():
            greet(me - 1, hd)

        @pl.when(me < n_seq - 1)
        def _():
            greet(me + 1, hd)

        @pl.when(z > 0)
        def _():
            greet(me - inner, hd)

        @pl.when(z < outer - 1)
        def _():
            greet(me + inner, hd)

        @pl.loop(0, heads)
        def _(h):
            in_copy(h).start()

        c_copy.start()

        @pl.when(me == 0)
        def _():
            left[...] = jnp.zeros(left.shape, BF16)

        @pl.when(me == n_seq - 1)
        def _():
            hrecv[...] = jnp.zeros(hrecv.shape, BF16)

        @pl.when(z == 0)
        def _():
            zrecv[0] = jnp.zeros(zrecv.shape[1:], BF16)

        @pl.when(z == outer - 1)
        def _():
            zrecv[1] = jnp.zeros(zrecv.shape[1:], BF16)

        xs[:, 0:RIM, :] = jnp.zeros((3, RIM, HEAD_DIM), F32)
        s_acc[...] = jnp.zeros(s_acc.shape, F32)
        i_acc[...] = jnp.zeros(i_acc.shape, F32)

        guests = inner - 1 + n_head - 1
        for there in (me > 0, me < n_seq - 1, z > 0, z < outer - 1):
            guests = guests + there.astype(jnp.int32)
        pl.semaphore_wait(bar, guests)

        left_copy = pltpu.make_async_remote_copy(
            src_ref=x_hbm.at[:, rows - RIM : rows, :],
            dst_ref=left,
            send_sem=lsem.at[0],
            recv_sem=lsem.at[1],
            device_id=(lax.rem(me + 1, n_seq), hd),
            device_id_type=MESH,
        )

        @pl.when(me < n_seq - 1)
        def _():
            left_copy.start()

        def conv_rows(i, h, count):
            total = w_ref[i, 0:1, col(h)] * xs[i, RIM : RIM + count, :]
            for j in range(1, taps):
                total = total + w_ref[i, j : j + 1, col(h)] * xs[i, RIM - j : RIM - j + count, :]
            return total.astype(BF16)

        @pl.loop(0, heads)
        def _(h):
            in_copy(h).wait()
            for i in (1, 2):
                xs[i, RIM : RIM + rows, :] = xin[i, :, col(h)].astype(F32)
                qkv[i, h] = conv_rows(i, h, rows)

        @pl.when(me > 0)
        def _():
            left_copy.wait_recv()

        def x_copy(way, d, h):
            return pltpu.make_async_remote_copy(
                src_ref=xsend.at[way, d - 1, h],
                dst_ref=xrecv.at[way, d - 1, h],
                send_sem=xsem_s.at[way, d - 1, h],
                recv_sem=xsem_r.at[way, d - 1, h],
                device_id=(peer_x(d), hd),
                device_id_type=MESH,
            )

        def z_copy(way, h):
            target = jnp.minimum(z + 1, outer - 1) if way == 0 else jnp.maximum(z - 1, 0)
            return pltpu.make_async_remote_copy(
                src_ref=zsend.at[way, h],
                dst_ref=zrecv.at[way, h],
                send_sem=zsem_s.at[way, h],
                recv_sem=zsem_r.at[way, h],
                device_id=(target * inner + x, hd),
                device_id_type=MESH,
            )

        has_prev = (z > 0, z < outer - 1)
        has_next = (z < outer - 1, z > 0)

        def scan_step(way, h):
            part = jnp.zeros((HEAD_DIM, HEAD_DIM), F32)
            total = own[h]
            for d in range(1, inner):
                x_copy(way, d, h).wait_recv()
                got = xrecv[way, d - 1, h].astype(F32)
                total = total + got
                before = (x >= d) if way == 0 else (x < d)
                part = part + got * before.astype(F32)

            @pl.when(has_prev[way])
            def _():
                z_copy(way, h).wait_recv()

            entering = zrecv[way, h].astype(F32)

            @pl.when(has_next[way])
            def _():
                zsend[way, h] = (entering + total).astype(BF16)
                z_copy(way, h).start()

            stb[way, h] = (entering + part).astype(BF16)

        def chain_step(way, h):
            @pl.when(has_prev[way])
            def _():
                z_copy(way, h).wait_recv()

            entering = zrecv[way, h].astype(F32)
            mine = own[h]

            @pl.when(has_next[way])
            def _():
                zsend[way, h] = (entering + mine).astype(BF16)
                z_copy(way, h).start()

            for d in range(1, inner):
                later = (x + d < inner) if way == 0 else (x + d >= inner)
                xsend[way, d - 1, h] = (entering + mine * later.astype(F32)).astype(BF16)
                x_copy(way, d, h).start()

        def join_step(way, h):
            entering = zrecv[way, h].astype(F32)
            for d in range(1, inner):
                x_copy(way, d, h).wait_recv()
                entering = entering + xrecv[way, d - 1, h].astype(F32)
            stb[way, h] = entering.astype(BF16)

        def is_odd(h):
            return lax.rem(h, 2) == 1

        def share(way, h, state):
            own[h] = state

            @pl.when(jnp.logical_not(is_odd(h)))
            def _():
                for d in range(1, inner):
                    xsend[way, d - 1, h] = state.astype(BF16)
                    x_copy(way, d, h).start()

            @pl.when(is_odd(h) & jnp.logical_not(has_prev[way]))
            def _():
                chain_step(way, h)

        far = (z, outer - 1 - z)
        lag = (
            jnp.where(far[0] == 0, 0, jnp.where(far[0] == 1, min(3, heads), heads)),
            jnp.where(far[1] == 0, 0, jnp.where(far[1] == 1, min(6, heads), heads)),
        )
        chain_lag = (
            jnp.clip(3 * far[0] - 1, 0, heads),
            jnp.where(far[1] <= 1, min(3, heads), heads),
        )

        def start_relay(way):
            @pl.when(jnp.logical_not(has_prev[way]))
            def _():
                @pl.loop(0, heads)
                def _(h):
                    @pl.when(jnp.logical_not(is_odd(h)))
                    def _():
                        scan_step(way, h)

        def relay_some(way, h):
            ha, hc = h - lag[way], h - chain_lag[way]

            @pl.when((hc >= 0) & is_odd(hc) & has_prev[way])
            def _():
                chain_step(way, hc)

            @pl.when((ha >= 0) & (lax.rem(ha, 2) == 0) & has_prev[way])
            def _():
                scan_step(way, ha)

        def relay_chains(way):
            @pl.loop(0, heads)
            def _(h):
                @pl.when((h >= heads - chain_lag[way]) & is_odd(h) & has_prev[way])
                def _():
                    chain_step(way, h)

        def finish(way, h):
            @pl.when((h >= heads - lag[way]) & jnp.logical_not(is_odd(h)))
            def _():
                scan_step(way, h)

            @pl.when(is_odd(h))
            def _():
                join_step(way, h)

        @pl.loop(0, heads)
        def _(h):
            for i in (1, 2):
                xs[i, 0:RIM, :] = left[i, :, col(h)].astype(F32)
                xs[i, RIM : RIM + TAIL, :] = xin[i, 0:TAIL, col(h)].astype(F32)
                qkv[i, h, 0:TAIL, :] = conv_rows(i, h, TAIL)
            share(0, h, dot(qkv[1, h], qkv[2, h], 0, 0))

        low0 = lower_mask(half, half, 0)
        low1 = lower_mask(half, rows, half)
        up0 = upper_mask(half, rows)
        up1 = upper_mask(half, half)

        start_relay(0)

        @pl.loop(0, heads)
        def _(h):
            xs[0, 0:RIM, :] = left[0, :, col(h)].astype(F32)
            xs[0, RIM : RIM + rows, :] = xin[0, :, col(h)].astype(F32)
            qkv[0, h] = conv_rows(0, h, rows)
            q0, q1 = qkv[0, h, 0:half, :], qkv[0, h, half:rows, :]
            k0, k1 = qkv[1, h, 0:half, :], qkv[1, h, half:rows, :]
            k, v, q = qkv[1, h], qkv[2, h], qkv[0, h]
            sc = jnp.where(low0, dot(q0, k0, 1, 1), 0.0).astype(BF16)
            att[h, 0:half, :] = dot(sc, v[0:half], 1, 0)
            sc = jnp.where(low1, dot(q1, k, 1, 1), 0.0).astype(BF16)
            att[h, half:rows, :] = dot(sc, v, 1, 0)
            scT[h, 0:half, :] = jnp.where(up0, dot(k0, q, 1, 1), 0.0).astype(BF16)
            scT[h, half:rows, half:rows] = jnp.where(up1, dot(k1, q1, 1, 1), 0.0).astype(BF16)

            relay_some(0, h)

        c_copy.wait()

        relay_chains(0)

        @pl.loop(0, heads)
        def _(h):
            finish(0, h)

            a = dot(qkv[0, h], stb[0, h], 1, 0) + att[h]
            att[h] = a
            s_acc[...] += a * a
            i_acc[...] += (gain_ref[:, col(h)] * cin[:, col(h)].astype(F32)) * a

        sums = []
        for acc in (s_acc, i_acc):
            for b in range(groups):
                piece = acc[b * HEAD_DIM : (b + 1) * HEAD_DIM, :].T
                sums.append(jnp.sum(piece, axis=0, keepdims=True))
        stat_s[...] = jnp.concatenate(sums, axis=0)

        def s_copy(d):
            return pltpu.make_async_remote_copy(
                src_ref=stat_s,
                dst_ref=stat_r.at[d - 1],
                send_sem=ssem_s.at[d - 1],
                recv_sem=ssem_r.at[d - 1],
                device_id=(me, peer_h(d)),
                device_id_type=MESH,
            )

        for d in range(1, n_head):
            s_copy(d).start()
        stats = stat_s[...]
        for d in range(1, n_head):
            s_copy(d).wait_recv()
            stats = stats + stat_r[d - 1]
        rms = jnp.sqrt(stats[0:groups] / width + 1e-05)
        inv = 1.0 / rms
        coef = stats[groups : 2 * groups] / (width * rms * rms * rms)
        turned = jnp.concatenate([inv, coef], axis=0).T
        for b in range(groups):
            at = slice(b * HEAD_DIM, (b + 1) * HEAD_DIM)
            rb[at, :] = jnp.broadcast_to(turned[:, b : b + 1], (HEAD_DIM, HEAD_DIM))
            cb[at, :] = jnp.broadcast_to(
                turned[:, groups + b : groups + b + 1], (HEAD_DIM, HEAD_DIM)
            )

        @pl.loop(0, heads)
        def _(h):
            weighted = gain_ref[:, col(h)] * cin[:, col(h)].astype(F32)
            g = (weighted * rb[...] - att[h] * cb[...]).astype(BF16)
            gb[h] = g
            share(1, h, dot(qkv[0, h], g, 0, 0))

        def out_copy(h):
            return pltpu.make_async_copy(outb.at[:, col(h)], out_hbm.at[:, col(h)], out_sem.at[h])

        start_relay(1)

        @pl.loop(0, heads)
        def _(h):
            outb[:, col(h)] = (gain_ref[:, col(h)] * att[h] * rb[...]).astype(BF16)
            out_copy(h).start()
            g, q, k, v = gb[h], qkv[0, h], qkv[1, h], qkv[2, h]
            across = dot(g, stb[0, h], 1, 1)
            m = jnp.where(low0, dot(g[0:half], v[0:half], 1, 1), 0.0).astype(BF16)
            gq[h, 0:half, :] = (across[0:half] + dot(m, k[0:half], 1, 0)).astype(BF16)
            m = jnp.where(low1, dot(g[half:rows], v, 1, 1), 0.0).astype(BF16)
            gq[h, half:rows, :] = (across[half:rows] + dot(m, k, 1, 0)).astype(BF16)
            m = jnp.where(up0, dot(v[0:half], g, 1, 1), 0.0).astype(BF16)
            gkv[0, h, 0:half, :] = dot(m, q, 1, 0)
            m = jnp.where(up1, dot(v[half:rows], g[half:rows], 1, 1), 0.0).astype(BF16)
            gkv[0, h, half:rows, :] = dot(m, q[half:rows], 1, 0)
            gkv[1, h, 0:half, :] = dot(scT[h, 0:half, :], g, 1, 0)
            gkv[1, h, half:rows, :] = dot(scT[h, half:rows, half:rows], g[half:rows], 1, 0)

            relay_some(1, h)

        def h_copy(h):
            return pltpu.make_async_remote_copy(
                src_ref=hsend.at[h],
                dst_ref=hrecv.at[h],
                send_sem=hsem_s.at[h],
                recv_sem=hsem_r.at[h],
                device_id=(jnp.maximum(me - 1, 0), hd),
                device_id_type=MESH,
            )

        body_rows = rows - TAIL

        def gi_copy(h):
            return pltpu.make_async_copy(
                gib.at[:, 0:body_rows, col(h)], gi_hbm.at[:, 0:body_rows, col(h)], gi_sem.at[h]
            )

        def back_rows(i, h, read, count):
            total = w_ref[i, 0:1, col(h)] * read(0, count)
            for j in range(1, taps):
                total = total + w_ref[i, j : j + 1, col(h)] * read(j, count)
            return total.astype(BF16)

        relay_chains(1)

        @pl.loop(0, heads)
        def _(h):
            finish(1, h)

            after = stb[1, h]
            gk = (gkv[0, h] + dot(qkv[2, h], after, 1, 1)).astype(BF16)
            gv = (gkv[1, h] + dot(qkv[1, h], after, 1, 0)).astype(BF16)
            for i, grad in enumerate((gq[h], gk, gv)):
                full = grad.astype(F32)
                xs[i, 0:rows, :] = full
                hsend[h, i] = xs[i, 0:RIM, :].astype(BF16)
                tail[h, i, 0:TAIL, :] = xs[i, rows - TAIL : rows, :]

            @pl.when(me > 0)
            def _():
                h_copy(h).start()

            for i in range(3):
                gib[i, 0:body_rows, col(h)] = back_rows(
                    i, h, lambda j, count, i=i: xs[i, j : j + count, :], body_rows
                )
            gi_copy(h).start()

        @pl.loop(0, heads)
        def _(h):
            @pl.when(me < n_seq - 1)
            def _():
                h_copy(h).wait_recv()

            for i in range(3):
                tail[h, i, TAIL : TAIL + RIM, :] = hrecv[h, i].astype(F32)
                gib[i, body_rows:rows, col(h)] = back_rows(
                    i, h, lambda j, count, i=i: tail[h, i, j : j + count, :], TAIL
                )

        tail_copy = pltpu.make_async_copy(
            gib.at[:, body_rows:rows, :], gi_hbm.at[:, body_rows:rows, :], tail_sem
        )
        tail_copy.start()

        @pl.when(me < n_seq - 1)
        def _():
            left_copy.wait_send()

        for d in range(1, n_head):
            s_copy(d).wait_send()

        @pl.loop(0, heads)
        def _(h):
            out_copy(h).wait()
            gi_copy(h).wait()
            for way in range(2):
                for d in range(1, inner):
                    x_copy(way, d, h).wait_send()

                @pl.when(has_next[way])
                def _():
                    z_copy(way, h).wait_send()

            @pl.when(me > 0)
            def _():
                h_copy(h).wait_send()

        tail_copy.wait()

    dma = pltpu.SemaphoreType.DMA
    state = (heads, HEAD_DIM, HEAD_DIM)
    scratch = [
        pltpu.VMEM((3, rows, cols), BF16),
        pltpu.VMEM((rows, cols), BF16),
        pltpu.VMEM((3, heads, rows, HEAD_DIM), BF16),
        pltpu.VMEM((3, rows + RIM, HEAD_DIM), F32),
        pltpu.VMEM((3, RIM, cols), BF16),
        pltpu.VMEM((heads, rows, rows), BF16),
        pltpu.VMEM((heads, rows, HEAD_DIM), F32),
        pltpu.VMEM((2,) + state, BF16),
        pltpu.VMEM((rows, HEAD_DIM), F32),
        pltpu.VMEM((rows, HEAD_DIM), F32),
        pltpu.VMEM((2 * groups, HEAD_DIM), F32),
        pltpu.VMEM((n_head - 1, 2 * groups, HEAD_DIM), F32),
        pltpu.VMEM((rows, HEAD_DIM), F32),
        pltpu.VMEM((rows, HEAD_DIM), F32),
        pltpu.VMEM((heads, rows, HEAD_DIM), BF16),
        pltpu.VMEM((rows, cols), BF16),
        pltpu.VMEM((heads, rows, HEAD_DIM), BF16),
        pltpu.VMEM((2, heads, rows, HEAD_DIM), F32),
        pltpu.VMEM((heads, 3, TAIL + RIM, HEAD_DIM), F32),
        pltpu.VMEM((3, rows, cols), BF16),
        pltpu.VMEM(state, F32),
        pltpu.VMEM((2, inner - 1) + state, BF16),
        pltpu.VMEM((2, inner - 1) + state, BF16),
        pltpu.VMEM((2,) + state, BF16),
        pltpu.VMEM((2,) + state, BF16),
        pltpu.VMEM((heads, 3, RIM, HEAD_DIM), BF16),
        pltpu.VMEM((heads, 3, RIM, HEAD_DIM), BF16),
        dma((heads,)),
        dma,
        dma((heads,)),
        dma((heads,)),
        dma,
        dma((2,)),
        dma((2, inner - 1, heads)),
        dma((2, inner - 1, heads)),
        dma((2, heads)),
        dma((2, heads)),
        dma((n_head - 1,)),
        dma((n_head - 1,)),
        dma((heads,)),
        dma((heads,)),
    ]
    return kernel, scratch


def place(output, grads, output_hbm, grads_hbm, sem):
    copies = [pltpu.make_async_copy(output, output_hbm, sem.at[3])]
    for i in range(3):
        copies.append(pltpu.make_async_copy(grads.at[i], grads_hbm.at[i], sem.at[i]))
    for copy in copies:
        copy.start()
    for copy in copies:
        copy.wait()


def solution(mesh):
    n_seq, n_head = mesh.shape["seq"], mesh.shape["head"]

    def body(inputs, conv_weight, gain, cotangent):
        _, rows, cols = inputs.shape
        assert rows == BLOCK and n_seq > 1 and n_head > 1
        kernel, scratch = make_kernel(n_seq, n_head, rows, cols, conv_weight.shape[1])
        anywhere = pl.BlockSpec(memory_space=pl.ANY)
        hbm = pl.BlockSpec(memory_space=pltpu.HBM)
        vmem = pl.BlockSpec(memory_space=pltpu.VMEM)
        shapes = (
            jax.ShapeDtypeStruct((rows, cols), BF16),
            jax.ShapeDtypeStruct((3, rows, cols), BF16),
        )
        output, grads = pl.pallas_call(
            kernel,
            out_shape=(pltpu.VMEM((rows, cols), BF16), pltpu.VMEM((3, rows, cols), BF16)),
            in_specs=[hbm, vmem, vmem, hbm],
            out_specs=(anywhere, anywhere),
            scratch_shapes=scratch,
            compiler_params=pltpu.CompilerParams(
                collective_id=0, has_side_effects=True, vmem_limit_bytes=58 * 1024 * 1024
            ),
            name="block",
        )(inputs, conv_weight, gain.reshape(1, cols), cotangent)
        return pl.pallas_call(
            place,
            out_shape=shapes,
            in_specs=[anywhere, anywhere],
            out_specs=(hbm, hbm),
            scratch_shapes=[pltpu.SemaphoreType.DMA((4,))],
            compiler_params=pltpu.CompilerParams(vmem_limit_bytes=1024 * 1024),
            name="place",
        )(output, grads)

    placed = (P(None, "seq", "head"), P(None, None, "head"), P("head"), P("seq", "head"))
    return jax.shard_map(
        body,
        mesh=mesh,
        in_specs=placed,
        out_specs=(P("seq", "head"), P(None, "seq", "head")),
        check_vma=False,
    )
```
